32 devices in a mesh: grp: 2 (over y), lat: 4 (over z), lay: 4 (over x, core).
Axes of the slice: x: 2, y: 2, z: 4, core: 2. Of those that a mesh axis runs over, the one named last changes fastest.
Arguments:
- acts: bfloat16 [128, 4, 1280], P(('grp', 'lat'), 'lay'), parts along dimension 0, may hold values from -6 to 6
- w_enc: bfloat16 [4, 1280, 1536], P('lay', None, 'lat'), may hold values from -0.078125 to 0.078125
- w_dec: bfloat16 [1536, 4, 1280], P('lat', 'lay'), may hold values from -0.15625 to 0.15625
- b_enc: float32 [1536], P('lat'), may hold values from -3 to 3
- b_dec: float32 [4, 1280], P('lay'), may hold values from -3 to 3
Outputs:
- lat_grad: bfloat16 [128, 1536], P('grp', 'lat'), parts along dimension 0
- enc_grad: bfloat16 [8, 1280, 1536], P(('grp', 'lay'), None, 'lat'), parts along dimension 0
- dec_grad: bfloat16 [1536, 8, 1280], P('lat', ('grp', 'lay')), parts along dimension 1
The draws below stay inside these ranges and needn't reach their ends.
There are 2 independent parts, one for each index of `grp`. The reference program is written for one: setup_inputs(seed, part) draws one part's arguments, and reference() takes and returns one part's arrays. A program takes and returns all parts, laid end to end along the dimension named above; an argument that names none is the same for every part. Nothing has to cross between parts.
All inputs are finite; a program needn't handle non-finite values.
Results may differ from the reference program's by a relative error of at most 0.023.
Values may be sent and summed in bfloat16 or wider, within the bound.
No kernel may reach another device: no remote copies, remote signals or barrier semaphores. Data moves between devices by JAX's collectives and lax.ppermute only.
A program may use at most 64 MiB of HBM per device.

```python
import jax
import jax.numpy as jnp

D = 1280
LATENTS = 1536
LAYERS = 4
ROWS = 64


def levels(stream_key, extent, pieces, least, top_value):
    def one(dim, parts):
        heights = jax.random.uniform(jax.random.fold_in(jax.random.fold_in(stream_key, 6), dim), (parts,), jnp.float32, least / len(pieces), top_value / len(pieces))
        return jnp.repeat(jnp.exp(heights), extent[dim] // parts).reshape((-1,) + (1,) * (len(extent) - dim - 1))

    level = one(*pieces[0])
    for cut in pieces[1:]:
        level = level * one(*cut)
    return level


def noise(key, dims, width, most, shards=(), held_as=jnp.bfloat16):
    array = width * jax.random.normal(key, dims, jnp.float32)
    if shards:
        array = array * levels(key, dims, shards, -0.22, 0.18)
    return jnp.clip(array, -most, most).astype(held_as)


def setup_inputs(seed: int = 0, part: int = 0) -> dict:
    streams_of = jax.random.split(jax.random.key(seed), 6)
    part_splits = jax.random.split(jax.random.fold_in(streams_of[5], part), 6)
    return {
        "acts": noise(part_splits[0], (ROWS, LAYERS, D), 1.0, 6.0, ((0, 4), (1, 4))),
        "w_enc": noise(streams_of[1], (LAYERS, D, LATENTS), (LAYERS * D) ** -0.5, 0.078125, ((0, 4), (2, 4))),
        "w_dec": noise(streams_of[2], (LATENTS, LAYERS, D), LATENTS ** -0.5, 0.15625, ((0, 4), (1, 4))),
        "b_enc": noise(streams_of[3], (LATENTS,), 0.5, 3.0, ((0, 4),), jnp.float32),
        "b_dec": noise(streams_of[4], (LAYERS, D), 0.5, 3.0, ((0, 4),), jnp.float32),
    }


def reference(acts, w_enc, w_dec, b_enc, b_dec):
    x32 = acts.astype(jnp.float32)
    pre = jnp.einsum("bld,ldm->bm", x32, w_enc.astype(jnp.float32)) + b_enc[None, :]
    code = (jax.nn.softplus(4.0 * pre) / 4.0).astype(jnp.bfloat16)
    slope = jax.nn.sigmoid(4.0 * pre)
    recon = jnp.einsum("bm,mld->bld", code.astype(jnp.float32), w_dec.astype(jnp.float32))
    err = (recon + b_dec[None, :, :] - x32).astype(jnp.bfloat16)
    back = jnp.einsum("bld,mld->bm", err.astype(jnp.float32), w_dec.astype(jnp.float32))
    lat_grad = (back * slope).astype(jnp.bfloat16)
    enc_grad = jnp.einsum("bld,bm->ldm", x32, lat_grad.astype(jnp.float32)).astype(jnp.bfloat16)
    dec_grad = jnp.einsum("bm,bld->mld", code.astype(jnp.float32), err.astype(jnp.float32)).astype(jnp.bfloat16)
    return lat_grad, enc_grad, dec_grad
```

```python
import jax
import jax.numpy as jnp
from jax import lax
from jax.sharding import PartitionSpec as P

DIRECT = 4


def direct(size):
    return size <= DIRECT and size & (size - 1) == 0


def swap(x, axis, size, step):
    return lax.ppermute(x, axis, [(a, a ^ step) for a in range(size)])


def gather_blocks(x, axis, size):
    return [x] + [swap(x, axis, size, k) for k in range(1, size)]


def pair_sum(terms):
    while len(terms) > 1:
        terms = [terms[k] + terms[k + 1] for k in range(0, len(terms), 2)]
    return terms[0]


def all_sum(x, axis, size):
    if not direct(size):
        return lax.psum(x, axis).astype(jnp.float32)
    return pair_sum([t.astype(jnp.float32) for t in gather_blocks(x, axis, size)])


def build(lat, lay):
    def on_device(acts, w_enc, w_dec, b_enc, b_dec):
        row_dev, lay_dev, width = acts.shape
        lat_dev = w_enc.shape[2]
        flat = lay_dev * width
        own = acts.reshape(row_dev, flat)
        we = w_enc.reshape(flat, lat_dev)
        wd = w_dec.reshape(lat_dev, flat)
        bd = b_dec.reshape(1, flat)
        near = direct(lat)
        if near:
            gathered = jnp.concatenate(gather_blocks(own, "lat", lat), axis=0)
        else:
            gathered = lax.all_gather(own, "lat", axis=0, tiled=True)
        term = jnp.dot(gathered, we, preferred_element_type=jnp.float32)
        pre = all_sum(term.astype(jnp.bfloat16), "lay", lay) + b_enc[None, :]
        code = (jax.nn.softplus(4.0 * pre) / 4.0).astype(jnp.bfloat16)
        slope = jax.nn.sigmoid(4.0 * pre)
        part = jnp.dot(code, wd, preferred_element_type=jnp.float32).astype(jnp.bfloat16)
        if near:
            pieces = part.reshape(lat, row_dev, flat)
            mine = pair_sum(
                [pieces[0].astype(jnp.float32)]
                + [swap(pieces[k], "lat", lat, k).astype(jnp.float32) for k in range(1, lat)]
            )
        else:
            mine = lax.psum_scatter(part, "lat", scatter_dimension=0, tiled=True).astype(jnp.float32)
        err_own = (mine + bd - own.astype(jnp.float32)).astype(jnp.bfloat16)
        if near:
            err = jnp.concatenate(gather_blocks(err_own, "lat", lat), axis=0)
        else:
            err = lax.all_gather(err_own, "lat", axis=0, tiled=True)
        back = lax.dot_general(err, wd, (((1,), (1,)), ((), ())), preferred_element_type=jnp.float32)
        total = all_sum(back.astype(jnp.bfloat16), "lay", lay)
        lat_grad = (total * slope).astype(jnp.bfloat16)
        enc_grad = lax.dot_general(
            gathered, lat_grad, (((0,), (0,)), ((), ())), preferred_element_type=jnp.float32
        ).astype(jnp.bfloat16)
        dec_grad = lax.dot_general(
            code, err, (((0,), (0,)), ((), ())), preferred_element_type=jnp.float32
        ).astype(jnp.bfloat16)
        if near:
            me = lax.axis_index("lat")
            blocks = lat_grad.reshape(lat, row_dev, lat_dev)
            lat_grad = jnp.concatenate(
                [lax.dynamic_index_in_dim(blocks, a ^ me, 0, keepdims=False) for a in range(lat)], axis=0
            )
        return (
            lat_grad,
            enc_grad.reshape(lay_dev, width, lat_dev),
            dec_grad.reshape(lat_dev, lay_dev, width),
        )

    return on_device


def solution(mesh):
    in_specs = (
        P(("grp", "lat"), "lay", None),
        P("lay", None, "lat"),
        P("lat", "lay", None),
        P("lat"),
        P("lay", None),
    )
    out_specs = (P("grp", "lat"), P(("grp", "lay"), None, "lat"), P("lat", ("grp", "lay"), None))
    return jax.shard_map(
        build(mesh.shape["lat"], mesh.shape["lay"]),
        mesh=mesh,
        in_specs=in_specs,
        out_specs=out_specs,
        check_vma=False,
    )
```

```python
import jax
import jax.numpy as jnp
from jax import lax
from jax.experimental import pallas as pl
from jax.experimental.pallas import tpu as pltpu
from jax.sharding import PartitionSpec as P


DIRECT = 4


def direct(size):
    return size <= DIRECT and size & (size - 1) == 0


def swap(x, axis, size, step):
    return lax.ppermute(x, axis, [(a, a ^ step) for a in range(size)])


def gather_blocks(x, axis, size):
    return [x] + [swap(x, axis, size, k) for k in range(1, size)]


def pair_sum(terms):
    while len(terms) > 1:
        terms = [terms[k] + terms[k + 1] for k in range(0, len(terms), 2)]
    return terms[0]


def all_sum(x, axis, size):
    if not direct(size):
        return lax.psum(x, axis).astype(jnp.float32)
    return pair_sum([t.astype(jnp.float32) for t in gather_blocks(x, axis, size)])


VMEM = pl.BlockSpec(memory_space=pltpu.VMEM)
HBM = pl.BlockSpec(memory_space=pltpu.HBM)
BLOCKS = 5
SMALL = pltpu.CompilerParams(vmem_limit_bytes=8 << 20)


def keep_near(*arrays):
    count = len(arrays)

    def kernel(*refs):
        sems = refs[-1]
        copies = [
            pltpu.make_async_copy(refs[n], refs[count + n], sems.at[n]) for n in range(count)
        ]
        for copy in copies:
            copy.start()
        for copy in copies:
            copy.wait()

    return pl.pallas_call(
        kernel,
        out_shape=[jax.ShapeDtypeStruct(a.shape, a.dtype) for a in arrays],
        in_specs=[HBM] * count,
        out_specs=[VMEM] * count,
        scratch_shapes=[pltpu.SemaphoreType.DMA((count,))],
        compiler_params=SMALL,
        name="keep_near",
    )(*[pltpu.with_memory_space_constraint(a, pltpu.HBM) for a in arrays])


def product(blocks, w):
    def kernel(*refs):
        *x_refs, w_ref, out_ref = refs
        x = jnp.concatenate([r[...] for r in x_refs], axis=0)
        out_ref[...] = jnp.dot(x, w_ref[...], preferred_element_type=jnp.float32).astype(out_ref.dtype)

    rows = sum(b.shape[0] for b in blocks)
    return pl.pallas_call(
        kernel,
        out_shape=jax.ShapeDtypeStruct((rows, w.shape[1]), jnp.bfloat16),
        in_specs=[VMEM] * (len(blocks) + 1),
        out_specs=VMEM,
        compiler_params=SMALL,
        name="product",
    )(*blocks, w)


def turned(blocks):
    def kernel(*refs):
        *x_refs, out_ref = refs
        out_ref[...] = jnp.concatenate([r[...] for r in x_refs], axis=0).T

    rows = sum(b.shape[0] for b in blocks)
    return pl.pallas_call(
        kernel,
        out_shape=jax.ShapeDtypeStruct((blocks[0].shape[1], rows), blocks[0].dtype),
        in_specs=[VMEM] * len(blocks),
        out_specs=VMEM,
        compiler_params=SMALL,
        name="turned",
    )(*blocks)


def last_stage(backs, slope, acts_t, lat):
    rows, lat_dev = slope.shape
    row_dev, depth = rows // lat, acts_t.shape[0]
    step = depth // BLOCKS
    count = len(backs)

    def kernel(*refs):
        b_refs, (slope_ref, x_ref, grad_ref, enc_ref, grad_held, held, sems) = (
            refs[:count],
            refs[count:],
        )
        total = pair_sum([r[...].astype(jnp.float32) for r in b_refs])
        grad = (total * slope_ref[...]).astype(jnp.bfloat16)
        me = lax.axis_index("lat")
        for k in range(lat):
            at = pl.multiple_of(lax.bitwise_xor(me, k) * row_dev, row_dev)
            grad_held[pl.ds(at, row_dev), :] = grad[k * row_dev : (k + 1) * row_dev]
        copies = [pltpu.make_async_copy(grad_held, grad_ref, sems.at[BLOCKS])]
        copies[0].start()
        for n in range(BLOCKS):
            part = pl.ds(n * step, step)
            held[part, :] = jnp.dot(
                x_ref[part, :], grad, preferred_element_type=jnp.float32
            ).astype(held.dtype)
            copies.append(pltpu.make_async_copy(held.at[part], enc_ref.at[part], sems.at[n]))
            copies[-1].start()
        for copy in copies:
            copy.wait()

    return pl.pallas_call(
        kernel,
        out_shape=(
            jax.ShapeDtypeStruct((rows, lat_dev), jnp.bfloat16),
            jax.ShapeDtypeStruct((depth, lat_dev), jnp.bfloat16),
        ),
        in_specs=[VMEM] * (count + 2),
        out_specs=(HBM, HBM),
        scratch_shapes=[
            pltpu.VMEM((rows, lat_dev), jnp.bfloat16),
            pltpu.VMEM((depth, lat_dev), jnp.bfloat16),
            pltpu.SemaphoreType.DMA((BLOCKS + 1,)),
        ],
        compiler_params=SMALL,
        name="last_stage",
    )(*backs, slope, acts_t)


def build(lat, lay):
    def step(acts, w_enc, w_dec, b_enc, b_dec):
        row_dev, lay_dev, width = acts.shape
        lat_dev = w_enc.shape[2]
        flat = lay_dev * width
        own = acts.reshape(row_dev, flat)
        we = w_enc.reshape(flat, lat_dev)
        wd = w_dec.reshape(lat_dev, flat)
        bd = b_dec.reshape(1, flat)
        near = direct(lat) and direct(lay)
        if near:
            blocks = gather_blocks(own, "lat", lat)
            blocks[0], we = keep_near(own, we)
            term = product(blocks, we)
            acts_t = turned(blocks)
            wd_t = turned([wd])
        else:
            gathered = lax.all_gather(own, "lat", axis=0, tiled=True)
            term = jnp.dot(gathered, we, preferred_element_type=jnp.float32)
        pre = all_sum(term.astype(jnp.bfloat16), "lay", lay) + b_enc[None, :]
        code = (jax.nn.softplus(4.0 * pre) / 4.0).astype(jnp.bfloat16)
        slope = jax.nn.sigmoid(4.0 * pre)
        part = jnp.dot(code, wd, preferred_element_type=jnp.float32).astype(jnp.bfloat16)
        if near:
            pieces = part.reshape(lat, row_dev, flat)
            mine = pair_sum(
                [pieces[0].astype(jnp.float32)]
                + [swap(pieces[k], "lat", lat, k).astype(jnp.float32) for k in range(1, lat)]
            )
        else:
            mine = lax.psum_scatter(part, "lat", scatter_dimension=0, tiled=True).astype(jnp.float32)
        err_own = (mine + bd - own.astype(jnp.float32)).astype(jnp.bfloat16)
        if near:
            errs = gather_blocks(err_own, "lat", lat)
            back = product(errs, wd_t)
            err = jnp.concatenate(errs, axis=0)
        else:
            err = lax.all_gather(err_own, "lat", axis=0, tiled=True)
            back = lax.dot_general(
                err, wd, (((1,), (1,)), ((), ())), preferred_element_type=jnp.float32
            ).astype(jnp.bfloat16)
        if near:
            lat_grad, enc_grad = last_stage(gather_blocks(back, "lay", lay), slope, acts_t, lat)
        else:
            lat_grad = (lax.psum(back, "lay").astype(jnp.float32) * slope).astype(jnp.bfloat16)
            enc_grad = lax.dot_general(
                gathered, lat_grad, (((0,), (0,)), ((), ())), preferred_element_type=jnp.float32
            ).astype(jnp.bfloat16)
        dec_grad = lax.dot_general(
            code, err, (((0,), (0,)), ((), ())), preferred_element_type=jnp.float32
        ).astype(jnp.bfloat16)
        return (
            lat_grad,
            enc_grad.reshape(lay_dev, width, lat_dev),
            dec_grad.reshape(lat_dev, lay_dev, width),
        )

    return step


def solution(mesh):
    in_specs = (
        P(("grp", "lat"), "lay", None),
        P("lay", None, "lat"),
        P("lat", "lay", None),
        P("lat"),
        P("lay", None),
    )
    out_specs = (P("grp", "lat"), P(("grp", "lay"), None, "lat"), P("lat", ("grp", "lay"), None))
    lat, lay = mesh.shape["lat"], mesh.shape["lay"]
    return jax.shard_map(
        build(lat, lay), mesh=mesh, in_specs=in_specs, out_specs=out_specs, check_vma=False
    )
```

```python
import jax
import jax.numpy as jnp
from jax import lax
from jax.experimental import pallas as pl
from jax.experimental.pallas import tpu as pltpu
from jax.sharding import PartitionSpec as P


DIRECT = 4


def direct(size):
    return 2 <= size <= DIRECT and size & (size - 1) == 0


def swap(x, axis, size, step):
    return lax.ppermute(x, axis, [(a, a ^ step) for a in range(size)])


def gather_blocks(x, axis, size):
    return [x] + [swap(x, axis, size, k) for k in range(1, size)]


def cross(x, lat, lay, step):
    pairs = [
        (a * lay + b, (a ^ step) * lay + (b ^ 1)) for a in range(lat) for b in range(lay)
    ]
    return lax.ppermute(x, ("lat", "lay"), pairs)


def pair_sum(terms):
    while len(terms) > 1:
        terms = [terms[k] + terms[k + 1] for k in range(0, len(terms), 2)]
    return terms[0]


VMEM = pl.BlockSpec(memory_space=pltpu.VMEM)
HBM = pl.BlockSpec(memory_space=pltpu.HBM)
BLOCKS = 5
SMALL = pltpu.CompilerParams(vmem_limit_bytes=8 << 20)


def keep_near(*arrays):
    count = len(arrays)

    def kernel(*refs):
        sems = refs[-1]
        copies = [
            pltpu.make_async_copy(refs[n], refs[count + n], sems.at[n]) for n in range(count)
        ]
        for copy in copies:
            copy.start()
        for copy in copies:
            copy.wait()

    return pl.pallas_call(
        kernel,
        out_shape=[jax.ShapeDtypeStruct(a.shape, a.dtype) for a in arrays],
        in_specs=[HBM] * count,
        out_specs=[VMEM] * count,
        scratch_shapes=[pltpu.SemaphoreType.DMA((count,))],
        compiler_params=SMALL,
        name="keep_near",
    )(*[pltpu.with_memory_space_constraint(a, pltpu.HBM) for a in arrays])


def product(blocks, w):
    def kernel(*refs):
        *x_refs, w_ref, out_ref = refs
        x = jnp.concatenate([r[...] for r in x_refs], axis=0)
        out_ref[...] = jnp.dot(x, w_ref[...], preferred_element_type=jnp.float32).astype(out_ref.dtype)

    rows = sum(b.shape[0] for b in blocks)
    return pl.pallas_call(
        kernel,
        out_shape=jax.ShapeDtypeStruct((rows, w.shape[1]), jnp.bfloat16),
        in_specs=[VMEM] * (len(blocks) + 1),
        out_specs=VMEM,
        compiler_params=SMALL,
        name="product",
    )(*blocks, w)


def turned(blocks):
    def kernel(*refs):
        *x_refs, out_ref = refs
        out_ref[...] = jnp.concatenate([r[...] for r in x_refs], axis=0).T

    rows = sum(b.shape[0] for b in blocks)
    return pl.pallas_call(
        kernel,
        out_shape=jax.ShapeDtypeStruct((blocks[0].shape[1], rows), blocks[0].dtype),
        in_specs=[VMEM] * len(blocks),
        out_specs=VMEM,
        compiler_params=SMALL,
        name="turned",
    )(*blocks)


def recon_pieces(terms, b_enc, wd, own, b_dec):
    count, (rows, lat_dev), (row_dev, width) = len(terms), terms[0].shape, own.shape

    def kernel(*refs):
        t_refs, (b_enc_ref, wd_ref, own_ref, b_dec_ref, code_ref, slope_ref), piece_refs = (
            refs[:count],
            refs[count : count + 6],
            refs[count + 6 :],
        )
        pre = pair_sum([r[...].astype(jnp.float32) for r in t_refs]) + b_enc_ref[...]
        x = 4.0 * pre
        soft = jnp.maximum(x, 0.0) + jnp.log1p(jnp.exp(-jnp.abs(x)))
        code = (soft * 0.25).astype(jnp.bfloat16)
        code_ref[...] = code
        slope_ref[...] = jax.nn.sigmoid(x)
        part = jnp.dot(code, wd_ref[...], preferred_element_type=jnp.float32)
        for k, ref in enumerate(piece_refs):
            piece = part[k * row_dev : (k + 1) * row_dev]
            if k == 0:
                piece = piece + b_dec_ref[...] - own_ref[...].astype(jnp.float32)
            ref[...] = piece.astype(jnp.bfloat16)

    pieces = rows // row_dev
    code, slope, *parts = pl.pallas_call(
        kernel,
        out_shape=[
            jax.ShapeDtypeStruct((rows, lat_dev), jnp.bfloat16),
            jax.ShapeDtypeStruct((rows, lat_dev), jnp.float32),
        ]
        + [jax.ShapeDtypeStruct((row_dev, width), jnp.bfloat16)] * pieces,
        in_specs=[VMEM] * (count + 4),
        out_specs=[VMEM] * (2 + pieces),
        compiler_params=SMALL,
        name="recon_pieces",
    )(*terms, b_enc, wd, own, b_dec)
    return code, slope, parts


def last_stage(backs, slope, acts_t, lat):
    rows, lat_dev = slope.shape
    row_dev, depth = rows // lat, acts_t.shape[0]
    step = depth // BLOCKS
    count = len(backs)

    def kernel(*refs):
        b_refs, (slope_ref, x_ref, grad_ref, enc_ref, grad_held, held, sems) = (
            refs[:count],
            refs[count:],
        )
        total = pair_sum([r[...].astype(jnp.float32) for r in b_refs])
        grad = (total * slope_ref[...]).astype(jnp.bfloat16)
        me = lax.axis_index("lat")
        for k in range(lat):
            at = pl.multiple_of(lax.bitwise_xor(me, k) * row_dev, row_dev)
            grad_held[pl.ds(at, row_dev), :] = grad[k * row_dev : (k + 1) * row_dev]
        copies = [pltpu.make_async_copy(grad_held, grad_ref, sems.at[BLOCKS])]
        copies[0].start()
        for n in range(BLOCKS):
            part = pl.ds(n * step, step)
            held[part, :] = jnp.dot(
                x_ref[part, :], grad, preferred_element_type=jnp.float32
            ).astype(held.dtype)
            copies.append(pltpu.make_async_copy(held.at[part], enc_ref.at[part], sems.at[n]))
            copies[-1].start()
        for copy in copies:
            copy.wait()

    return pl.pallas_call(
        kernel,
        out_shape=(
            jax.ShapeDtypeStruct((rows, lat_dev), jnp.bfloat16),
            jax.ShapeDtypeStruct((depth, lat_dev), jnp.bfloat16),
        ),
        in_specs=[VMEM] * (count + 2),
        out_specs=(HBM, HBM),
        scratch_shapes=[
            pltpu.VMEM((rows, lat_dev), jnp.bfloat16),
            pltpu.VMEM((depth, lat_dev), jnp.bfloat16),
            pltpu.SemaphoreType.DMA((BLOCKS + 1,)),
        ],
        compiler_params=SMALL,
        name="last_stage",
    )(*backs, slope, acts_t)


def near_step(lat, lay):
    def step(own, we, wd, b_enc, b_dec):
        blocks = gather_blocks(own, "lat", lat)
        blocks[0], we = keep_near(own, we)
        terms = gather_blocks(product(blocks, we), "lay", lay)
        acts_t = turned(blocks)
        code, slope, parts = recon_pieces(terms, b_enc, wd, blocks[0], b_dec)
        err_own = pair_sum(
            [cross(p, lat, lay, k).astype(jnp.float32) for k, p in enumerate(parts)]
        ).astype(jnp.bfloat16)
        wd_t = turned([wd])
        errs = [cross(err_own, lat, lay, k) for k in range(lat)]
        backs = gather_blocks(product(errs, wd_t), "lay", lay)
        lat_grad, enc_grad = last_stage(backs, slope, acts_t, lat)
        return lat_grad, enc_grad, code, jnp.concatenate(errs, axis=0)

    return step


def far_step(own, we, wd, b_enc, b_dec):
    gathered = lax.all_gather(own, "lat", axis=0, tiled=True)
    term = jnp.dot(gathered, we, preferred_element_type=jnp.float32)
    pre = lax.psum(term.astype(jnp.bfloat16), "lay").astype(jnp.float32) + b_enc
    code = (jax.nn.softplus(4.0 * pre) / 4.0).astype(jnp.bfloat16)
    slope = jax.nn.sigmoid(4.0 * pre)
    part = jnp.dot(code, wd, preferred_element_type=jnp.float32).astype(jnp.bfloat16)
    mine = lax.psum_scatter(part, "lat", scatter_dimension=0, tiled=True).astype(jnp.float32)
    err_own = (mine + b_dec - own.astype(jnp.float32)).astype(jnp.bfloat16)
    err = lax.all_gather(err_own, "lat", axis=0, tiled=True)
    back = lax.dot_general(err, wd, (((1,), (1,)), ((), ())), preferred_element_type=jnp.float32)
    back = lax.psum(back.astype(jnp.bfloat16), "lay").astype(jnp.float32)
    lat_grad = (back * slope).astype(jnp.bfloat16)
    enc_grad = lax.dot_general(
        gathered, lat_grad, (((0,), (0,)), ((), ())), preferred_element_type=jnp.float32
    ).astype(jnp.bfloat16)
    return lat_grad, enc_grad, code, err


def build(step):
    def on_device(acts, w_enc, w_dec, b_enc, b_dec):
        row_dev, lay_dev, width = acts.shape
        lat_dev = w_enc.shape[2]
        flat = lay_dev * width
        lat_grad, enc_grad, code, err = step(
            acts.reshape(row_dev, flat),
            w_enc.reshape(flat, lat_dev),
            w_dec.reshape(lat_dev, flat),
            b_enc.reshape(1, lat_dev),
            b_dec.reshape(1, flat),
        )
        dec_grad = lax.dot_general(
            code, err, (((0,), (0,)), ((), ())), preferred_element_type=jnp.float32
        ).astype(jnp.bfloat16)
        return (
            lat_grad,
            enc_grad.reshape(lay_dev, width, lat_dev),
            dec_grad.reshape(lat_dev, lay_dev, width),
        )

    return on_device


def solution(mesh):
    in_specs = (
        P(("grp", "lat"), "lay", None),
        P("lay", None, "lat"),
        P("lat", "lay", None),
        P("lat"),
        P("lay", None),
    )
    out_specs = (P("grp", "lat"), P(("grp", "lay"), None, "lat"), P("lat", ("grp", "lay"), None))
    lat, lay = mesh.shape["lat"], mesh.shape["lay"]
    near = direct(lat) and direct(lay)
    return jax.shard_map(
        build(near_step(lat, lay) if near else far_step),
        mesh=mesh,
        in_specs=in_specs,
        out_specs=out_specs,
        check_vma=False,
    )
```

```python
import jax
import jax.numpy as jnp
from jax import lax
from jax.experimental import pallas as pl
from jax.experimental.pallas import tpu as pltpu
from jax.sharding import PartitionSpec as P


DIRECT = 4


def direct(size):
    return 2 <= size <= DIRECT and size & (size - 1) == 0


def swap(x, axis, size, step):
    return lax.ppermute(x, axis, [(a, a ^ step) for a in range(size)])


def gather_blocks(x, axis, size):
    return [x] + [swap(x, axis, size, k) for k in range(1, size)]


def cross(x, lat, lay, step):
    pairs = [
        (a * lay + b, (a ^ step) * lay + (b ^ 1)) for a in range(lat) for b in range(lay)
    ]
    return lax.ppermute(x, ("lat", "lay"), pairs)


def pair_sum(terms):
    while len(terms) > 1:
        terms = [terms[k] + terms[k + 1] for k in range(0, len(terms), 2)]
    return terms[0]


VMEM = pl.BlockSpec(memory_space=pltpu.VMEM)
HBM = pl.BlockSpec(memory_space=pltpu.HBM)
BLOCKS = 5
SMALL = pltpu.CompilerParams(vmem_limit_bytes=8 << 20)


def keep_near(*arrays):
    count = len(arrays)

    def kernel(*refs):
        sems = refs[-1]
        copies = [
            pltpu.make_async_copy(refs[n], refs[count + n], sems.at[n]) for n in range(count)
        ]
        for copy in copies:
            copy.start()
        for copy in copies:
            copy.wait()

    return pl.pallas_call(
        kernel,
        out_shape=[jax.ShapeDtypeStruct(a.shape, a.dtype) for a in arrays],
        in_specs=[HBM] * count,
        out_specs=[VMEM] * count,
        scratch_shapes=[pltpu.SemaphoreType.DMA((count,))],
        compiler_params=SMALL,
        name="keep_near",
    )(*[pltpu.with_memory_space_constraint(a, pltpu.HBM) for a in arrays])


def product(blocks, w):
    def kernel(*refs):
        *x_refs, w_ref, out_ref = refs
        x = jnp.concatenate([r[...] for r in x_refs], axis=0)
        out_ref[...] = jnp.dot(x, w_ref[...], preferred_element_type=jnp.float32).astype(out_ref.dtype)

    rows = sum(b.shape[0] for b in blocks)
    return pl.pallas_call(
        kernel,
        out_shape=jax.ShapeDtypeStruct((rows, w.shape[1]), jnp.bfloat16),
        in_specs=[VMEM] * (len(blocks) + 1),
        out_specs=VMEM,
        compiler_params=SMALL,
        name="product",
    )(*blocks, w)


def turned(blocks):
    def kernel(*refs):
        *x_refs, out_ref = refs
        out_ref[...] = jnp.concatenate([r[...] for r in x_refs], axis=0).T

    rows = sum(b.shape[0] for b in blocks)
    return pl.pallas_call(
        kernel,
        out_shape=jax.ShapeDtypeStruct((blocks[0].shape[1], rows), blocks[0].dtype),
        in_specs=[VMEM] * len(blocks),
        out_specs=VMEM,
        compiler_params=SMALL,
        name="turned",
    )(*blocks)


def recon_pieces(terms, b_enc, wd, own, b_dec):
    count, (rows, lat_dev), (row_dev, width) = len(terms), terms[0].shape, own.shape

    def kernel(*refs):
        t_refs, (b_enc_ref, wd_ref, own_ref, b_dec_ref, code_ref, slope_ref), piece_refs = (
            refs[:count],
            refs[count : count + 6],
            refs[count + 6 :],
        )
        pre = pair_sum([r[...].astype(jnp.float32) for r in t_refs]) + b_enc_ref[...]
        x = 4.0 * pre
        small = jnp.exp(-jnp.abs(x))
        soft = jnp.maximum(x, 0.0) + jnp.log1p(small)
        code = (soft * 0.25).astype(jnp.bfloat16)
        code_ref[...] = code
        slope_ref[...] = jnp.where(x >= 0.0, 1.0, small) / (1.0 + small)
        part = jnp.dot(code, wd_ref[...], preferred_element_type=jnp.float32)
        for k, ref in enumerate(piece_refs):
            piece = part[k * row_dev : (k + 1) * row_dev]
            if k == 0:
                piece = piece + b_dec_ref[...] - own_ref[...].astype(jnp.float32)
            ref[...] = piece.astype(jnp.bfloat16)

    pieces = rows // row_dev
    code, slope, *parts = pl.pallas_call(
        kernel,
        out_shape=[
            jax.ShapeDtypeStruct((rows, lat_dev), jnp.bfloat16),
            jax.ShapeDtypeStruct((rows, lat_dev), jnp.float32),
        ]
        + [jax.ShapeDtypeStruct((row_dev, width), jnp.bfloat16)] * pieces,
        in_specs=[VMEM] * (count + 4),
        out_specs=[VMEM] * (2 + pieces),
        compiler_params=SMALL,
        name="recon_pieces",
    )(*terms, b_enc, wd, own, b_dec)
    return code, slope, parts


def last_stage(backs, slope, acts_t, lat):
    rows, lat_dev = slope.shape
    row_dev, depth = rows // lat, acts_t.shape[0]
    parts = BLOCKS if depth % (16 * BLOCKS) == 0 else 1
    step = depth // parts
    count = len(backs)

    def kernel(*refs):
        b_refs, (slope_ref, x_ref, grad_ref, enc_ref, grad_held, held, sems) = (
            refs[:count],
            refs[count:],
        )
        total = pair_sum([r[...].astype(jnp.float32) for r in b_refs])
        grad = (total * slope_ref[...]).astype(jnp.bfloat16)
        me = lax.axis_index("lat")
        for k in range(lat):
            at = pl.multiple_of(lax.bitwise_xor(me, k) * row_dev, row_dev)
            grad_held[pl.ds(at, row_dev), :] = grad[k * row_dev : (k + 1) * row_dev]
        copies = [pltpu.make_async_copy(grad_held, grad_ref, sems.at[parts])]
        copies[0].start()
        for n in range(parts):
            part = pl.ds(n * step, step)
            held[part, :] = jnp.dot(
                x_ref[part, :], grad, preferred_element_type=jnp.float32
            ).astype(held.dtype)
            copies.append(pltpu.make_async_copy(held.at[part], enc_ref.at[part], sems.at[n]))
            copies[-1].start()
        for copy in copies:
            copy.wait()

    return pl.pallas_call(
        kernel,
        out_shape=(
            jax.ShapeDtypeStruct((rows, lat_dev), jnp.bfloat16),
            jax.ShapeDtypeStruct((depth, lat_dev), jnp.bfloat16),
        ),
        in_specs=[VMEM] * (count + 2),
        out_specs=(HBM, HBM),
        scratch_shapes=[
            pltpu.VMEM((rows, lat_dev), jnp.bfloat16),
            pltpu.VMEM((depth, lat_dev), jnp.bfloat16),
            pltpu.SemaphoreType.DMA((parts + 1,)),
        ],
        compiler_params=SMALL,
        name="last_stage",
    )(*backs, slope, acts_t)


def near_step(lat, lay):
    def step(own, we, wd, b_enc, b_dec):
        blocks = gather_blocks(own, "lat", lat)
        blocks[0], we = keep_near(own, we)
        terms = gather_blocks(product(blocks, we), "lay", lay)
        acts_t = turned(blocks)
        code, slope, parts = recon_pieces(terms, b_enc, wd, blocks[0], b_dec)
        err_own = pair_sum(
            [cross(p, lat, lay, k).astype(jnp.float32) for k, p in enumerate(parts)]
        ).astype(jnp.bfloat16)
        wd_t = turned([wd])
        errs = [cross(err_own, lat, lay, k) for k in range(lat)]
        backs = gather_blocks(product(errs, wd_t), "lay", lay)
        lat_grad, enc_grad = last_stage(backs, slope, acts_t, lat)
        return lat_grad, enc_grad, code, jnp.concatenate(errs, axis=0)

    return step


def far_step(own, we, wd, b_enc, b_dec):
    gathered = lax.all_gather(own, "lat", axis=0, tiled=True)
    term = jnp.dot(gathered, we, preferred_element_type=jnp.float32)
    pre = lax.psum(term.astype(jnp.bfloat16), "lay").astype(jnp.float32) + b_enc
    code = (jax.nn.softplus(4.0 * pre) / 4.0).astype(jnp.bfloat16)
    slope = jax.nn.sigmoid(4.0 * pre)
    part = jnp.dot(code, wd, preferred_element_type=jnp.float32).astype(jnp.bfloat16)
    mine = lax.psum_scatter(part, "lat", scatter_dimension=0, tiled=True).astype(jnp.float32)
    err_own = (mine + b_dec - own.astype(jnp.float32)).astype(jnp.bfloat16)
    err = lax.all_gather(err_own, "lat", axis=0, tiled=True)
    back = lax.dot_general(err, wd, (((1,), (1,)), ((), ())), preferred_element_type=jnp.float32)
    back = lax.psum(back.astype(jnp.bfloat16), "lay").astype(jnp.float32)
    lat_grad = (back * slope).astype(jnp.bfloat16)
    enc_grad = lax.dot_general(
        gathered, lat_grad, (((0,), (0,)), ((), ())), preferred_element_type=jnp.float32
    ).astype(jnp.bfloat16)
    return lat_grad, enc_grad, code, err


def build(step):
    def on_device(acts, w_enc, w_dec, b_enc, b_dec):
        row_dev, lay_dev, width = acts.shape
        lat_dev = w_enc.shape[2]
        flat = lay_dev * width
        lat_grad, enc_grad, code, err = step(
            acts.reshape(row_dev, flat),
            w_enc.reshape(flat, lat_dev),
            w_dec.reshape(lat_dev, flat),
            b_enc.reshape(1, lat_dev),
            b_dec.reshape(1, flat),
        )
        dec_grad = lax.dot_general(
            code, err, (((0,), (0,)), ((), ())), preferred_element_type=jnp.float32
        ).astype(jnp.bfloat16)
        return (
            lat_grad,
            enc_grad.reshape(lay_dev, width, lat_dev),
            dec_grad.reshape(lat_dev, lay_dev, width),
        )

    return on_device


def solution(mesh):
    in_specs = (
        P(("grp", "lat"), "lay", None),
        P("lay", None, "lat"),
        P("lat", "lay", None),
        P("lat"),
        P("lay", None),
    )
    out_specs = (P("grp", "lat"), P(("grp", "lay"), None, "lat"), P("lat", ("grp", "lay"), None))
    lat, lay = mesh.shape["lat"], mesh.shape["lay"]
    near = direct(lat) and direct(lay)
    return jax.shard_map(
        build(near_step(lat, lay) if near else far_step),
        mesh=mesh,
        in_specs=in_specs,
        out_specs=out_specs,
        check_vma=False,
    )
```

```python
import jax
import jax.numpy as jnp
from jax import lax
from jax.experimental import pallas as pl
from jax.experimental.pallas import tpu as pltpu
from jax.sharding import PartitionSpec as P


DIRECT = 4


def direct(size):
    return 2 <= size <= DIRECT and size & (size - 1) == 0


def swap(x, axis, size, step):
    return lax.ppermute(x, axis, [(a, a ^ step) for a in range(size)])


def gather_blocks(x, axis, size):
    return [x] + [swap(x, axis, size, k) for k in range(1, size)]


def cross(x, lat, lay, step):
    pairs = [
        (a * lay + b, (a ^ step) * lay + (b ^ 1)) for a in range(lat) for b in range(lay)
    ]
    return lax.ppermute(x, ("lat", "lay"), pairs)


def pair_sum(terms):
    while len(terms) > 1:
        terms = [terms[k] + terms[k + 1] for k in range(0, len(terms), 2)]
    return terms[0]


VMEM = pl.BlockSpec(memory_space=pltpu.VMEM)
HBM = pl.BlockSpec(memory_space=pltpu.HBM)
BLOCKS = 5
SMALL = pltpu.CompilerParams(vmem_limit_bytes=8 << 20)
TIGHT = pltpu.CompilerParams(vmem_limit_bytes=8 << 20)


def keep_near(*arrays):
    count = len(arrays)

    def kernel(*refs):
        sems = refs[-1]
        copies = [
            pltpu.make_async_copy(refs[n], refs[count + n], sems.at[n]) for n in range(count)
        ]
        for copy in copies:
            copy.start()
        for copy in copies:
            copy.wait()

    return pl.pallas_call(
        kernel,
        out_shape=[jax.ShapeDtypeStruct(a.shape, a.dtype) for a in arrays],
        in_specs=[HBM] * count,
        out_specs=[VMEM] * count,
        scratch_shapes=[pltpu.SemaphoreType.DMA((count,))],
        compiler_params=SMALL,
        name="keep_near",
    )(*[pltpu.with_memory_space_constraint(a, pltpu.HBM) for a in arrays])


def product(blocks, w):
    def kernel(*refs):
        *x_refs, w_ref, out_ref = refs
        x = jnp.concatenate([r[...] for r in x_refs], axis=0)
        out_ref[...] = jnp.dot(x, w_ref[...], preferred_element_type=jnp.float32).astype(out_ref.dtype)

    rows = sum(b.shape[0] for b in blocks)
    return pl.pallas_call(
        kernel,
        out_shape=jax.ShapeDtypeStruct((rows, w.shape[1]), jnp.bfloat16),
        in_specs=[VMEM] * (len(blocks) + 1),
        out_specs=VMEM,
        compiler_params=TIGHT,
        name="product",
    )(*blocks, w)


def turned(blocks):
    def kernel(*refs):
        *x_refs, out_ref = refs
        out_ref[...] = jnp.concatenate([r[...] for r in x_refs], axis=0).T

    rows = sum(b.shape[0] for b in blocks)
    return pl.pallas_call(
        kernel,
        out_shape=jax.ShapeDtypeStruct((blocks[0].shape[1], rows), blocks[0].dtype),
        in_specs=[VMEM] * len(blocks),
        out_specs=VMEM,
        compiler_params=SMALL,
        name="turned",
    )(*blocks)


def recon_pieces(terms, b_enc, wd, own, b_dec):
    count, (rows, lat_dev), (row_dev, width) = len(terms), terms[0].shape, own.shape

    def kernel(*refs):
        t_refs, (b_enc_ref, wd_ref, own_ref, b_dec_ref, code_ref, scaled_ref), piece_refs = (
            refs[:count],
            refs[count : count + 6],
            refs[count + 6 :],
        )
        pre = pair_sum([r[...].astype(jnp.float32) for r in t_refs]) + b_enc_ref[...]
        x = 4.0 * pre
        small = jnp.exp(-jnp.abs(x))
        soft = jnp.maximum(x, 0.0) + jnp.log1p(small)
        code = (soft * 0.25).astype(jnp.bfloat16)
        code_ref[...] = code
        scaled_ref[...] = x
        part = jnp.dot(code, wd_ref[...], preferred_element_type=jnp.float32)
        for k, ref in enumerate(piece_refs):
            piece = part[k * row_dev : (k + 1) * row_dev]
            if k == 0:
                piece = piece + b_dec_ref[...] - own_ref[...].astype(jnp.float32)
            ref[...] = piece.astype(jnp.bfloat16)

    pieces = rows // row_dev
    code, scaled, *parts = pl.pallas_call(
        kernel,
        out_shape=[
            jax.ShapeDtypeStruct((rows, lat_dev), jnp.bfloat16),
            jax.ShapeDtypeStruct((rows, lat_dev), jnp.float32),
        ]
        + [jax.ShapeDtypeStruct((row_dev, width), jnp.bfloat16)] * pieces,
        in_specs=[VMEM] * (count + 4),
        out_specs=[VMEM] * (2 + pieces),
        compiler_params=SMALL,
        name="recon_pieces",
    )(*terms, b_enc, wd, own, b_dec)
    return code, scaled, parts


def last_stage(backs, slope, acts_t, lat):
    rows, lat_dev = slope.shape
    row_dev, depth = rows // lat, acts_t.shape[0]
    parts = BLOCKS if depth % (16 * BLOCKS) == 0 else 1
    step = depth // parts
    count = len(backs)

    def kernel(*refs):
        b_refs, (slope_ref, x_ref, grad_ref, enc_ref, grad_held, held, sems) = (
            refs[:count],
            refs[count:],
        )
        total = pair_sum([r[...].astype(jnp.float32) for r in b_refs])
        grad = (total * slope_ref[...]).astype(jnp.bfloat16)
        me = lax.axis_index("lat")
        for k in range(lat):
            at = pl.multiple_of(lax.bitwise_xor(me, k) * row_dev, row_dev)
            grad_held[pl.ds(at, row_dev), :] = grad[k * row_dev : (k + 1) * row_dev]
        copies = [pltpu.make_async_copy(grad_held, grad_ref, sems.at[parts])]
        copies[0].start()
        for n in range(parts):
            part = pl.ds(n * step, step)
            held[part, :] = jnp.dot(
                x_ref[part, :], grad, preferred_element_type=jnp.float32
            ).astype(held.dtype)
            copies.append(pltpu.make_async_copy(held.at[part], enc_ref.at[part], sems.at[n]))
            copies[-1].start()
        for copy in copies:
            copy.wait()

    return pl.pallas_call(
        kernel,
        out_shape=(
            jax.ShapeDtypeStruct((rows, lat_dev), jnp.bfloat16),
            jax.ShapeDtypeStruct((depth, lat_dev), jnp.bfloat16),
        ),
        in_specs=[VMEM] * (count + 2),
        out_specs=(HBM, HBM),
        scratch_shapes=[
            pltpu.VMEM((rows, lat_dev), jnp.bfloat16),
            pltpu.VMEM((depth, lat_dev), jnp.bfloat16),
            pltpu.SemaphoreType.DMA((parts + 1,)),
        ],
        compiler_params=TIGHT,
        name="last_stage",
    )(*backs, slope, acts_t)


def near_step(lat, lay):
    def step(own, we, wd, b_enc, b_dec):
        blocks = gather_blocks(own, "lat", lat)
        blocks[0], we = keep_near(own, we)
        terms = gather_blocks(product(blocks, we), "lay", lay)
        acts_t = turned(blocks)
        code, scaled, parts = recon_pieces(terms, b_enc, wd, blocks[0], b_dec)
        err_own = pair_sum(
            [cross(p, lat, lay, k).astype(jnp.float32) for k, p in enumerate(parts)]
        ).astype(jnp.bfloat16)
        wd_t = turned([wd])
        slope = jax.nn.sigmoid(scaled)
        errs = [cross(err_own, lat, lay, k) for k in range(lat)]
        backs = gather_blocks(product(errs, wd_t), "lay", lay)
        lat_grad, enc_grad = last_stage(backs, slope, acts_t, lat)
        return lat_grad, enc_grad, code, jnp.concatenate(errs, axis=0)

    return step


def far_step(own, we, wd, b_enc, b_dec):
    gathered = lax.all_gather(own, "lat", axis=0, tiled=True)
    term = jnp.dot(gathered, we, preferred_element_type=jnp.float32)
    pre = lax.psum(term.astype(jnp.bfloat16), "lay").astype(jnp.float32) + b_enc
    code = (jax.nn.softplus(4.0 * pre) / 4.0).astype(jnp.bfloat16)
    slope = jax.nn.sigmoid(4.0 * pre)
    part = jnp.dot(code, wd, preferred_element_type=jnp.float32).astype(jnp.bfloat16)
    mine = lax.psum_scatter(part, "lat", scatter_dimension=0, tiled=True).astype(jnp.float32)
    err_own = (mine + b_dec - own.astype(jnp.float32)).astype(jnp.bfloat16)
    err = lax.all_gather(err_own, "lat", axis=0, tiled=True)
    back = lax.dot_general(err, wd, (((1,), (1,)), ((), ())), preferred_element_type=jnp.float32)
    back = lax.psum(back.astype(jnp.bfloat16), "lay").astype(jnp.float32)
    lat_grad = (back * slope).astype(jnp.bfloat16)
    enc_grad = lax.dot_general(
        gathered, lat_grad, (((0,), (0,)), ((), ())), preferred_element_type=jnp.float32
    ).astype(jnp.bfloat16)
    return lat_grad, enc_grad, code, err


def build(step):
    def on_device(acts, w_enc, w_dec, b_enc, b_dec):
        row_dev, lay_dev, width = acts.shape
        lat_dev = w_enc.shape[2]
        flat = lay_dev * width
        lat_grad, enc_grad, code, err = step(
            acts.reshape(row_dev, flat),
            w_enc.reshape(flat, lat_dev),
            w_dec.reshape(lat_dev, flat),
            b_enc.reshape(1, lat_dev),
            b_dec.reshape(1, flat),
        )
        dec_grad = lax.dot_general(
            code, err, (((0,), (0,)), ((), ())), preferred_element_type=jnp.float32
        ).astype(jnp.bfloat16)
        return (
            lat_grad,
            enc_grad.reshape(lay_dev, width, lat_dev),
            dec_grad.reshape(lat_dev, lay_dev, width),
        )

    return on_device


def solution(mesh):
    in_specs = (
        P(("grp", "lat"), "lay", None),
        P("lay", None, "lat"),
        P("lat", "lay", None),
        P("lat"),
        P("lay", None),
    )
    out_specs = (P("grp", "lat"), P(("grp", "lay"), None, "lat"), P("lat", ("grp", "lay"), None))
    lat, lay = mesh.shape["lat"], mesh.shape["lay"]
    near = direct(lat) and direct(lay)
    return jax.shard_map(
        build(near_step(lat, lay) if near else far_step),
        mesh=mesh,
        in_specs=in_specs,
        out_specs=out_specs,
        check_vma=False,
    )
```

```python
import jax
import jax.numpy as jnp
from jax import lax
from jax.experimental import pallas as pl
from jax.experimental.pallas import tpu as pltpu
from jax.sharding import PartitionSpec as P


DIRECT = 4


def direct(size):
    return 2 <= size <= DIRECT and size & (size - 1) == 0


def swap(x, axis, size, step):
    return lax.ppermute(x, axis, [(a, a ^ step) for a in range(size)])


def gather_blocks(x, axis, size):
    return [x] + [swap(x, axis, size, k) for k in range(1, size)]


def cross(x, lat, lay, step):
    pairs = [
        (a * lay + b, (a ^ step) * lay + (b ^ 1)) for a in range(lat) for b in range(lay)
    ]
    return lax.ppermute(x, ("lat", "lay"), pairs)


def pair_sum(terms):
    while len(terms) > 1:
        terms = [terms[k] + terms[k + 1] for k in range(0, len(terms), 2)]
    return terms[0]


VMEM = pl.BlockSpec(memory_space=pltpu.VMEM)
HBM = pl.BlockSpec(memory_space=pltpu.HBM)
BLOCKS = (1, 3, 3, 2, 1)
SMALL = pltpu.CompilerParams(vmem_limit_bytes=8 << 20)
TIGHT = pltpu.CompilerParams(vmem_limit_bytes=8 << 20)


def keep_near(*arrays):
    count = len(arrays)

    def kernel(*refs):
        sems = refs[-1]
        copies = [
            pltpu.make_async_copy(refs[n], refs[count + n], sems.at[n]) for n in range(count)
        ]
        for copy in copies:
            copy.start()
        for copy in copies:
            copy.wait()

    return pl.pallas_call(
        kernel,
        out_shape=[jax.ShapeDtypeStruct(a.shape, a.dtype) for a in arrays],
        in_specs=[HBM] * count,
        out_specs=[VMEM] * count,
        scratch_shapes=[pltpu.SemaphoreType.DMA((count,))],
        compiler_params=SMALL,
        name="keep_near",
    )(*[pltpu.with_memory_space_constraint(a, pltpu.HBM) for a in arrays])


def product(blocks, w):
    def kernel(*refs):
        *x_refs, w_ref, out_ref = refs
        x = jnp.concatenate([r[...] for r in x_refs], axis=0)
        out_ref[...] = jnp.dot(x, w_ref[...], preferred_element_type=jnp.float32).astype(out_ref.dtype)

    rows = sum(b.shape[0] for b in blocks)
    return pl.pallas_call(
        kernel,
        out_shape=jax.ShapeDtypeStruct((rows, w.shape[1]), jnp.bfloat16),
        in_specs=[VMEM] * (len(blocks) + 1),
        out_specs=VMEM,
        compiler_params=TIGHT,
        name="product",
    )(*blocks, w)


def turned(blocks):
    def kernel(*refs):
        *x_refs, out_ref = refs
        out_ref[...] = jnp.concatenate([r[...] for r in x_refs], axis=0).T

    rows = sum(b.shape[0] for b in blocks)
    return pl.pallas_call(
        kernel,
        out_shape=jax.ShapeDtypeStruct((blocks[0].shape[1], rows), blocks[0].dtype),
        in_specs=[VMEM] * len(blocks),
        out_specs=VMEM,
        compiler_params=SMALL,
        name="turned",
    )(*blocks)


def recon_pieces(terms, b_enc, wd, own, b_dec):
    count, (rows, lat_dev), (row_dev, width) = len(terms), terms[0].shape, own.shape

    def kernel(*refs):
        t_refs, (b_enc_ref, wd_ref, own_ref, b_dec_ref, code_ref, scaled_ref), piece_refs = (
            refs[:count],
            refs[count : count + 6],
            refs[count + 6 :],
        )
        pre = pair_sum([r[...].astype(jnp.float32) for r in t_refs]) + b_enc_ref[...]
        x = 4.0 * pre
        small = jnp.exp(-jnp.abs(x))
        soft = jnp.maximum(x, 0.0) + jnp.log1p(small)
        code = (soft * 0.25).astype(jnp.bfloat16)
        code_ref[...] = code
        scaled_ref[...] = x
        part = jnp.dot(code, wd_ref[...], preferred_element_type=jnp.float32)
        for k, ref in enumerate(piece_refs):
            piece = part[k * row_dev : (k + 1) * row_dev]
            if k == 0:
                piece = piece + b_dec_ref[...] - own_ref[...].astype(jnp.float32)
            ref[...] = piece.astype(jnp.bfloat16)

    pieces = rows // row_dev
    code, scaled, *parts = pl.pallas_call(
        kernel,
        out_shape=[
            jax.ShapeDtypeStruct((rows, lat_dev), jnp.bfloat16),
            jax.ShapeDtypeStruct((rows, lat_dev), jnp.float32),
        ]
        + [jax.ShapeDtypeStruct((row_dev, width), jnp.bfloat16)] * pieces,
        in_specs=[VMEM] * (count + 4),
        out_specs=[VMEM] * (2 + pieces),
        compiler_params=SMALL,
        name="recon_pieces",
    )(*terms, b_enc, wd, own, b_dec)
    return code, scaled, parts


def last_stage(backs, slope, acts_t, lat):
    rows, lat_dev = slope.shape
    row_dev, depth = rows // lat, acts_t.shape[0]
    shares = BLOCKS if depth % (16 * sum(BLOCKS)) == 0 else (1,)
    parts, unit = len(shares), depth // sum(shares)
    count = len(backs)

    def kernel(*refs):
        b_refs, (slope_ref, x_ref, grad_ref, enc_ref, grad_held, held, sems) = (
            refs[:count],
            refs[count:],
        )
        total = pair_sum([r[...].astype(jnp.float32) for r in b_refs])
        grad = (total * slope_ref[...]).astype(jnp.bfloat16)
        me = lax.axis_index("lat")
        for k in range(lat):
            at = pl.multiple_of(lax.bitwise_xor(me, k) * row_dev, row_dev)
            grad_held[pl.ds(at, row_dev), :] = grad[k * row_dev : (k + 1) * row_dev]
        copies = [pltpu.make_async_copy(grad_held, grad_ref, sems.at[parts])]
        copies[0].start()
        for n in range(parts):
            part = pl.ds(sum(shares[:n]) * unit, shares[n] * unit)
            held[part, :] = jnp.dot(
                x_ref[part, :], grad, preferred_element_type=jnp.float32
            ).astype(held.dtype)
            copies.append(pltpu.make_async_copy(held.at[part], enc_ref.at[part], sems.at[n]))
            copies[-1].start()
        for copy in copies:
            copy.wait()

    return pl.pallas_call(
        kernel,
        out_shape=(
            jax.ShapeDtypeStruct((rows, lat_dev), jnp.bfloat16),
            jax.ShapeDtypeStruct((depth, lat_dev), jnp.bfloat16),
        ),
        in_specs=[VMEM] * (count + 2),
        out_specs=(HBM, HBM),
        scratch_shapes=[
            pltpu.VMEM((rows, lat_dev), jnp.bfloat16),
            pltpu.VMEM((depth, lat_dev), jnp.bfloat16),
            pltpu.SemaphoreType.DMA((parts + 1,)),
        ],
        compiler_params=TIGHT,
        name="last_stage",
    )(*backs, slope, acts_t)


def near_step(lat, lay):
    def step(own, we, wd, b_enc, b_dec):
        blocks = gather_blocks(own, "lat", lat)
        blocks[0], we = keep_near(own, we)
        terms = gather_blocks(product(blocks, we), "lay", lay)
        acts_t = turned(blocks)
        code, scaled, parts = recon_pieces(terms, b_enc, wd, blocks[0], b_dec)
        err_own = pair_sum(
            [cross(p, lat, lay, k).astype(jnp.float32) for k, p in enumerate(parts)]
        ).astype(jnp.bfloat16)
        wd_t = turned([wd])
        slope = jax.nn.sigmoid(scaled)
        errs = [cross(err_own, lat, lay, k) for k in range(lat)]
        backs = gather_blocks(product(errs, wd_t), "lay", lay)
        lat_grad, enc_grad = last_stage(backs, slope, acts_t, lat)
        return lat_grad, enc_grad, code, jnp.concatenate(errs, axis=0)

    return step


def far_step(own, we, wd, b_enc, b_dec):
    gathered = lax.all_gather(own, "lat", axis=0, tiled=True)
    term = jnp.dot(gathered, we, preferred_element_type=jnp.float32)
    pre = lax.psum(term.astype(jnp.bfloat16), "lay").astype(jnp.float32) + b_enc
    code = (jax.nn.softplus(4.0 * pre) / 4.0).astype(jnp.bfloat16)
    slope = jax.nn.sigmoid(4.0 * pre)
    part = jnp.dot(code, wd, preferred_element_type=jnp.float32).astype(jnp.bfloat16)
    mine = lax.psum_scatter(part, "lat", scatter_dimension=0, tiled=True).astype(jnp.float32)
    err_own = (mine + b_dec - own.astype(jnp.float32)).astype(jnp.bfloat16)
    err = lax.all_gather(err_own, "lat", axis=0, tiled=True)
    back = lax.dot_general(err, wd, (((1,), (1,)), ((), ())), preferred_element_type=jnp.float32)
    back = lax.psum(back.astype(jnp.bfloat16), "lay").astype(jnp.float32)
    lat_grad = (back * slope).astype(jnp.bfloat16)
    enc_grad = lax.dot_general(
        gathered, lat_grad, (((0,), (0,)), ((), ())), preferred_element_type=jnp.float32
    ).astype(jnp.bfloat16)
    return lat_grad, enc_grad, code, err


def build(step):
    def on_device(acts, w_enc, w_dec, b_enc, b_dec):
        row_dev, lay_dev, width = acts.shape
        lat_dev = w_enc.shape[2]
        flat = lay_dev * width
        lat_grad, enc_grad, code, err = step(
            acts.reshape(row_dev, flat),
            w_enc.reshape(flat, lat_dev),
            w_dec.reshape(lat_dev, flat),
            b_enc.reshape(1, lat_dev),
            b_dec.reshape(1, flat),
        )
        dec_grad = lax.dot_general(
            code, err, (((0,), (0,)), ((), ())), preferred_element_type=jnp.float32
        ).astype(jnp.bfloat16)
        return (
            lat_grad,
            enc_grad.reshape(lay_dev, width, lat_dev),
            dec_grad.reshape(lat_dev, lay_dev, width),
        )

    return on_device


def solution(mesh):
    in_specs = (
        P(("grp", "lat"), "lay", None),
        P("lay", None, "lat"),
        P("lat", "lay", None),
        P("lat"),
        P("lay", None),
    )
    out_specs = (P("grp", "lat"), P(("grp", "lay"), None, "lat"), P("lat", ("grp", "lay"), None))
    lat, lay = mesh.shape["lat"], mesh.shape["lay"]
    near = direct(lat) and direct(lay)
    return jax.shard_map(
        build(near_step(lat, lay) if near else far_step),
        mesh=mesh,
        in_specs=in_specs,
        out_specs=out_specs,
        check_vma=False,
    )
```
